512 devices in a mesh: pair: 32 (over y, x), row: 16 (over z, core).
Axes of the slice: x: 4, y: 8, z: 8, core: 2. Of those that a mesh axis runs over, the one named last changes fastest.
Arguments:
- matrix: float32 [2048, 32768], P('pair', 'row')
Outputs:
- rotated: float32 [2048, 32768], P('pair', 'row')
- accumulated: float32 [2048, 2048], P('pair', 'row')
All inputs are finite; a program needn't handle non-finite values.
Results may differ from the reference program's by a relative error of at most 0.015.
Values sent between devices are 32-bit elements; how exact they have to be, the bound alone decides.
A program may use at most 64 MiB of HBM per device.

```python
import math
import jax
import jax.numpy as jnp
import numpy as np
from jax import lax

BW = 32
ROUNDS = 2
COLS = 2048
ROWS = 32768
N_PAIR = 32


def draw_matrix(key, part):
    base_key = jax.random.fold_in(key, 7)
    first, second = jax.random.split(base_key, 2)
    levels = jax.random.permutation(second, COLS).astype(jnp.float32)
    jitter = jax.random.uniform(jax.random.fold_in(second, 3), (COLS,), jnp.float32, -0.2, 0.2)
    scales = jnp.exp(math.log(10.0) * (levels + 0.5 + jitter) / COLS)
    values = jax.random.normal(first, (ROWS, COLS), jnp.float32)
    return (values * scales[None, :] / math.sqrt(ROWS)).T


def setup_inputs(seed: int = 0) -> dict:
    key_of = jax.random.split(jax.random.key(seed), 2)
    matrix = draw_matrix(jax.random.fold_in(key_of[1], 71), 0)
    return {"matrix": matrix}


def sweep_tables(width):
    others = list(range(1, width))
    first = []
    second = []
    partner = []
    sides = []
    for step in range(width - 1):
        order = [0] + others[step:] + others[:step]
        left = [order[i] for i in range(width // 2)]
        right = [order[width - 1 - i] for i in range(width // 2)]
        mate = [0] * width
        sign = [0.0] * width
        for a, b in zip(left, right):
            mate[a] = b
            mate[b] = a
            sign[a] = 1.0
            sign[b] = -1.0
        first.append(left)
        second.append(right)
        partner.append(mate)
        sides.append(sign)
    return (np.array(first, dtype=np.int32), np.array(second, dtype=np.int32), np.array(partner, dtype=np.int32), np.array(sides, dtype=np.float32))

def turn_matrix(gram):
    width = gram.shape[0]
    first, second, partner, sides = sweep_tables(width)
    counter = jnp.arange(width, dtype=jnp.int32)
    identity = (counter[:, None] == counter[None, :]).astype(gram.dtype)
    high = lax.Precision.HIGHEST

    def step(carry, indices):
        current, product = carry
        left, right, mate, side = indices
        left_hot = (counter[:, None] == left[None, :]).astype(gram.dtype)
        right_hot = (counter[:, None] == right[None, :]).astype(gram.dtype)
        g_pp = current[left, left]
        g_qq = current[right, right]
        g_pq = current[left, right]
        differ = g_qq - g_pp
        signum = jnp.where(differ >= 0, 1.0, -1.0).astype(gram.dtype)
        tangent = 2.0 * g_pq * signum / (jnp.abs(differ) + jnp.sqrt(differ * differ + 4.0 * g_pq * g_pq))
        cosine = 1.0 / jnp.sqrt(1.0 + tangent * tangent)
        sine = cosine * tangent
        both_hot = left_hot + right_hot
        cos_index = lax.optimization_barrier(jnp.sum(both_hot * cosine[None, :], axis=1))
        sin_index = lax.optimization_barrier(jnp.sum(both_hot * sine[None, :], axis=1)) * side.astype(gram.dtype)
        mate_hot = (mate[:, None] == counter[None, :]).astype(gram.dtype)
        plane = identity * cos_index[:, None] + mate_hot * sin_index[:, None]
        current = jnp.dot(plane.T, jnp.dot(current, plane, precision=high), precision=high)
        product = jnp.dot(product, plane, precision=high)
        return ((current, product), None)
    start = (gram, identity)
    tables = (jnp.asarray(first), jnp.asarray(second), jnp.asarray(partner), jnp.asarray(sides))
    (final, product), unused = lax.scan(step, start, tables)
    return product

def slot_source(count):
    source = np.zeros(2 * count, dtype=np.int32)
    source[0] = 0
    source[2] = 1
    for k in range(2, count):
        source[2 * k] = 2 * (k - 1)
    source[2 * count - 1] = 2 * (count - 1)
    for k in range(count - 1):
        source[2 * k + 1] = 2 * (k + 1) + 1
    return source

def reference(matrix):
    current = matrix.T
    rows_all, cols_all = current.shape
    width = 2 * BW
    high = lax.Precision.HIGHEST
    source = jnp.asarray(slot_source(N_PAIR))
    basis = jnp.eye(cols_all, dtype=matrix.dtype)
    for rnd in range(ROUNDS):
        blocks = current.reshape(rows_all, N_PAIR, width)
        vblocks = basis.reshape(cols_all, N_PAIR, width)
        gram = jnp.einsum('rkc,rkd->kcd', blocks, blocks, precision=high)
        turns = jax.vmap(turn_matrix)(gram)
        blocks = jnp.einsum('rkc,kcd->rkd', blocks, turns, precision=high)
        vblocks = jnp.einsum('rkc,kcd->rkd', vblocks, turns, precision=high)
        if rnd + 1 < ROUNDS:
            blocks = jnp.take(blocks.reshape(rows_all, 2 * N_PAIR, BW), source, axis=1)
            vblocks = jnp.take(vblocks.reshape(cols_all, 2 * N_PAIR, BW), source, axis=1)
        current = blocks.reshape(rows_all, cols_all)
        basis = vblocks.reshape(cols_all, cols_all)
    return (current.T, basis.T)
```

```python
import functools

import jax
import jax.numpy as jnp
from jax import lax
from jax.experimental import pallas as pl
from jax.experimental.pallas import tpu as pltpu
from jax.sharding import PartitionSpec as P

ROUNDS = 2
F32 = jnp.float32
HIGH = lax.Precision.HIGHEST
MESH = pl.DeviceIdType.MESH

def lane_gather(x, idx):
    return jnp.take_along_axis(x, idx, axis=1, mode="promise_in_bounds")

def iota(shape, d):
    return lax.broadcasted_iota(jnp.int32, shape, d)

def sweep_consts():
    lane = iota((8, 128), 1)
    sub = iota((8, 128), 0)
    j = lane & 63
    is_v = j >= 32
    is_l = lane < 32
    left = jnp.where(j == 0, 0, jnp.where(j == 31, 95, j + 1))
    right = jnp.where(j == 0, 1, lane - 1)
    pi = jnp.where(is_v, lane, jnp.where(is_l, left, right))
    pp = jnp.where(is_v, lane, pi ^ 64)
    sign = jnp.where(pi < 64, -1.0, 1.0).astype(F32)
    pair = jnp.where(is_v, 127, pi & 63)
    hots = []
    for v in range(4):
        hots.append(jnp.where(pair == v + 4 * sub, 1.0, 0.0).astype(F32))
    vone = jnp.where(is_v, 1.0, 0.0).astype(F32)
    return lane, sub, pi, pp, sign, hots, vone

def angle(gpp, gqq, gpq):
    d = gqq - gpp
    ad = jnp.abs(d)
    b = 2.0 * gpq
    small = jnp.maximum(ad, jnp.abs(b)) < 1e-15
    k = jnp.where(small, F32(2.0 ** 100), F32(1.0))
    ad = ad * k
    b = b * k
    h = ad * ad + b * b
    r = h * lax.rsqrt(h)
    hu = 0.5 * (ad + r)
    w = lax.rsqrt(r * hu)
    c = hu * w
    s = (0.5 * b) * jnp.where(d >= 0, w, -w)
    return c, s

def ssum(x):
    x = x + pltpu.roll(x, 4, 0)
    x = x + pltpu.roll(x, 2, 0)
    return x + pltpu.roll(x, 1, 0)

def make_step(consts):
    lane, sub, pi, pp, sign, hots, vone = consts
    def step(_, carry):
        P, Q = list(carry[:4]), list(carry[4:])
        c, s = [], []
        for v in range(4):
            ip = v + 4 * sub
            gpp = lane_gather(P[v], ip)
            gpq = lane_gather(P[v], ip + 64)
            gqq = lane_gather(Q[v], ip + 64)
            cv, sv = angle(gpp, gqq, gpq)
            c.append(cv); s.append(sv)
        cc = ssum((c[0] * hots[0] + c[1] * hots[1]) + (c[2] * hots[2] + c[3] * hots[3])) + vone
        sc = ssum((s[0] * hots[0] + s[1] * hots[1]) + (s[2] * hots[2] + s[3] * hots[3])) * sign
        P2, Q2 = [], []
        for v in range(4):
            pa = lane_gather(P[v], pi); pb = lane_gather(P[v], pp)
            qa = lane_gather(Q[v], pi); qb = lane_gather(Q[v], pp)
            P2.append((c[v] * pa - s[v] * qa) * cc + (c[v] * pb - s[v] * qb) * sc)
            Q2.append((s[v] * pa + c[v] * qa) * cc + (s[v] * pb + c[v] * qb) * sc)
        up = pltpu.roll(P2[0], 7, 0)
        dn = pltpu.roll(Q2[3], 1, 0)
        Pn = [jnp.where(sub == 0, P2[0], P2[1]), P2[2], P2[3], jnp.where(sub == 7, Q2[3], up)]
        Qn = [jnp.where(sub == 0, P2[1], dn), Q2[0], Q2[1], Q2[2]]
        return tuple(Pn + Qn)
    return step

def row_perm():
    r = iota((64, 64), 0)
    n = iota((64, 64), 1)
    q = r >= 32
    rr = r & 31
    i = (rr >> 3) + 4 * (rr & 7)
    idx = jnp.where(q, 63 - i, i)
    return jnp.where(n == idx, 1.0, 0.0).astype(F32)

def col_perm():
    n = iota((64, 128), 0)
    l = iota((64, 128), 1)
    j = l & 63
    idx = jnp.where(l < 64, j, 63 - j)
    return jnp.where((j < 32) & (n == idx), 1.0, 0.0).astype(F32)

def v_start():
    r = iota((64, 128), 0)
    l = iota((64, 128), 1)
    rr = r & 31
    i = (rr >> 3) + 4 * (rr & 7)
    idx = jnp.where(r >= 32, 63 - i, i)
    j = l & 63
    n = jnp.where(l < 64, j - 32, j)
    return jnp.where((j >= 32) & (n == idx), 1.0, 0.0).astype(F32)

def v_cols():
    l = iota((128, 64), 0)
    n = iota((128, 64), 1)
    j = l & 63
    m = jnp.where(l < 64, j - 32, j)
    return jnp.where((j >= 32) & (m == n), 1.0, 0.0).astype(F32)

def dot(a, b):
    return jnp.dot(a, b, precision=HIGH, preferred_element_type=F32)

def dot_ta(a, b):
    return lax.dot_general(a, b, (((0,), (0,)), ((), ())), precision=HIGH, preferred_element_type=F32)

def sweep(gram, unroll=1):
    rp = row_perm()
    state = dot(dot(rp, gram), col_perm()) + v_start()
    carry = tuple(state[8 * v: 8 * v + 8] for v in range(8))
    step = make_step(sweep_consts())
    carry = lax.fori_loop(0, 63, step, carry, unroll=unroll)
    state = jnp.concatenate(carry, axis=0)
    return dot(dot_ta(rp, state), v_cols())


def gram_of(a, b):
    dims = (((1,), (1,)), ((), ()))
    ah = a.astype(jnp.bfloat16)
    al = (a - ah.astype(F32)).astype(jnp.bfloat16)
    bh = b.astype(jnp.bfloat16)
    bl = (b - bh.astype(F32)).astype(jnp.bfloat16)
    out = lax.dot_general(ah, bh, dims, preferred_element_type=F32)
    out += lax.dot_general(ah, bl, dims, preferred_element_type=F32)
    return out + lax.dot_general(al, bh, dims, preferred_element_type=F32)


def pack(g):
    return jnp.concatenate([g[:32], g[32:]], axis=1)


def unpack(p):
    return jnp.concatenate([p[:, :64], p[:, 64:]], axis=0)


def send(src, dst, sems, slot, device):
    return pltpu.make_async_remote_copy(
        src_ref=src, dst_ref=dst, send_sem=sems[0].at[slot], recv_sem=sems[1].at[slot],
        device_id=device, device_id_type=MESH)


def turn_kernel(x_ref, t_ref, part, mate, chips, send_sem, recv_sem):
    pair = lax.axis_index("pair")
    row = lax.axis_index("row")
    z = row // 2
    core = row % 2
    partner = (pair, 2 * z + (1 - core))
    others = [(pair, 2 * ((z + d) % 8) + core) for d in range(1, 8)]
    barrier = pltpu.get_barrier_semaphore()
    for dev in [partner] + others:
        pl.semaphore_signal(barrier, inc=1, device_id=dev, device_id_type=MESH)
    x = x_ref[...]
    part[...] = pack(gram_of(x, x))
    pl.semaphore_wait(barrier, 8)
    sems = (send_sem, recv_sem)
    copy = send(part, mate, sems, 0, partner)
    copy.start()
    copy.wait()
    chips[z] = part[...] + mate[...]
    copies = [send(chips.at[z], chips.at[z], sems, d, others[d - 1]) for d in range(1, 8)]
    for copy in copies:
        copy.start()
    for copy in copies:
        copy.wait()
    total = ((chips[0] + chips[1]) + (chips[2] + chips[3])) + ((chips[4] + chips[5]) + (chips[6] + chips[7]))
    t_ref[...] = sweep(unpack(total))


def turn_of(columns):
    vmem = pl.BlockSpec(memory_space=pltpu.VMEM)
    return pl.pallas_call(
        turn_kernel,
        out_shape=jax.ShapeDtypeStruct((64, 64), F32),
        in_specs=[vmem],
        out_specs=vmem,
        scratch_shapes=[
            pltpu.VMEM((32, 128), F32),
            pltpu.VMEM((32, 128), F32),
            pltpu.VMEM((8, 32, 128), F32),
            pltpu.SemaphoreType.DMA((8,)),
            pltpu.SemaphoreType.DMA((8,)),
        ],
        compiler_params=pltpu.CompilerParams(collective_id=0, has_side_effects=True),
    )(columns)


def from_behind(array, axis, by):
    devices = lax.axis_size(axis)
    pairs = [(i, i + by) for i in range(devices) if 0 <= i + by < devices]
    return lax.ppermute(array, axis, pairs)


def local(matrix):
    pair_count = lax.axis_size("pair")
    row_count = lax.axis_size("row")
    pair_index = lax.axis_index("pair")
    row_index = lax.axis_index("row")
    width, local_rows = matrix.shape
    half = width // 2
    basis_rows = width * pair_count // row_count
    global_row = row_index * basis_rows + jnp.arange(basis_rows, dtype=jnp.int32)
    global_col = pair_index * width + jnp.arange(width, dtype=jnp.int32)
    basis = (global_col[:, None] == global_row[None, :]).astype(matrix.dtype)
    columns = matrix
    for rnd in range(ROUNDS):
        turn_t = turn_of(columns)
        stacked = jnp.concatenate([columns, basis], axis=1)
        stacked = jnp.dot(turn_t, stacked, precision=HIGH)
        if rnd + 1 < ROUNDS:
            upper = stacked[:half]
            lower = stacked[half:]
            outgoing = jnp.where(pair_index == 0, lower, upper)
            came_forward = from_behind(outgoing, "pair", 1)
            came_backward = from_behind(lower, "pair", -1)
            new_upper = jnp.where(pair_index == 0, upper, came_forward)
            new_lower = jnp.where(pair_index == pair_count - 1, upper, came_backward)
            stacked = jnp.concatenate([new_upper, new_lower], axis=0)
        columns = stacked[:, :local_rows]
        basis = stacked[:, local_rows:]
    return (columns, basis)


def solution(mesh):
    in_specs = (P("pair", "row"),)
    out_specs = (P("pair", "row"), P("pair", "row"))
    return jax.shard_map(local, mesh=mesh, in_specs=in_specs, out_specs=out_specs, check_vma=False)
```

```python
import jax
import jax.numpy as jnp
from jax import lax
from jax.experimental import pallas as pl
from jax.experimental.pallas import tpu as pltpu
from jax.sharding import PartitionSpec as P

F32 = jnp.float32
BF16 = jnp.bfloat16
HIGH = lax.Precision.HIGHEST
MESH = pl.DeviceIdType.MESH
STEPS = 63
BREAK_1 = 36
BREAK_2 = 48


def iota(shape, d):
    return lax.broadcasted_iota(jnp.int32, shape, d)


def lane_gather(x, idx):
    dims = lax.GatherDimensionNumbers(
        offset_dims=(), collapsed_slice_dims=(1,), start_index_map=(1,),
        operand_batching_dims=(0,), start_indices_batching_dims=(0,))
    return lax.gather(x, idx[..., None], dims, (1, 1), mode=lax.GatherScatterMode.PROMISE_IN_BOUNDS)


def dot(a, b):
    return jnp.dot(a, b, precision=HIGH, preferred_element_type=F32)


def dot_tn(a, b):
    return lax.dot_general(a, b, (((0,), (0,)), ((), ())), precision=HIGH, preferred_element_type=F32)


def dot_nt(a, b):
    return lax.dot_general(a, b, (((1,), (1,)), ((), ())), precision=HIGH, preferred_element_type=F32)


def angle(gpp, gqq, gpq):
    d = gqq - gpp
    ad = jnp.abs(d)
    small = jnp.maximum(ad, jnp.abs(gpq)) < 1e-15
    k = jnp.where(small, F32(2.0 ** 100), F32(1.0))
    ad = ad * k
    g = gpq * k
    b = g + g
    h = ad * ad + b * b
    r = h * lax.rsqrt(h)
    hu = 0.5 * (ad + r)
    w = lax.rsqrt(r * hu)
    c = hu * w
    s = g * jnp.where(d >= 0, w, -w)
    return c, s, s * (r * w) * gpq


def ssum(x):
    x = x + pltpu.roll(x, 4, 0)
    x = x + pltpu.roll(x, 2, 0)
    return x + pltpu.roll(x, 1, 0)


def shift(p, q, first, last):
    up = pltpu.roll(p[0], 7, 0)
    down = pltpu.roll(q[3], 1, 0)
    new_p = [jnp.where(first, p[0], p[1]), p[2], p[3], jnp.where(last, q[3], up)]
    new_q = [jnp.where(first, p[1], down), q[0], q[1], q[2]]
    return new_p, new_q


def step(_, carry):
    lane = iota((8, 128), 1)
    sub = iota((8, 128), 0)
    first, last = sub == 0, sub == 7
    wide = lane >= 64
    p, q, dp, dq, rq = [list(carry[4 * n:4 * n + 4]) for n in range(5)]
    pos, mate = carry[20], carry[21]
    near = jnp.where(wide, 127, jnp.minimum(pos, 63 - pos))
    sign = jnp.where(pos < 32, -1.0, 1.0).astype(F32)
    partner = jnp.where(mate == lane, 0, mate)
    partner = jnp.where(wide, lane, partner)
    c, s, cs, ss = [], [], [], []
    for v in range(4):
        cv, sv, fix = angle(dp[v], dq[v], lane_gather(p[v], rq[v]))
        dp[v] = dp[v] - fix
        dq[v] = dq[v] + fix
        hit = near == v + 4 * sub
        c.append(cv)
        s.append(sv)
        cs.append(jnp.where(hit, cv, 0.0))
        ss.append(jnp.where(hit, sv, 0.0))
    cc = ssum((cs[0] + cs[1]) + (cs[2] + cs[3])) + jnp.where(wide, 1.0, 0.0)
    sc = ssum((ss[0] + ss[1]) + (ss[2] + ss[3])) * sign
    for v in range(4):
        pm = lane_gather(p[v], partner)
        qm = lane_gather(q[v], partner)
        a, b = p[v], q[v]
        p[v] = (c[v] * a - s[v] * b) * cc + (c[v] * pm - s[v] * qm) * sc
        q[v] = (s[v] * a + c[v] * b) * cc + (s[v] * pm + c[v] * qm) * sc
    p, q = shift(p, q, first, last)
    dp, dq = shift(dp, dq, first, last)
    rq = [jnp.where(x == 63, 1, x + 1) for x in rq]
    pos = jnp.where(pos == 0, 0, jnp.where(pos == 1, 63, pos - 1))
    mate = mate + jnp.where(lane == 0, 1, 2)
    mate = jnp.where(mate > 63, mate - 63, mate)
    return tuple(p + q + dp + dq + rq + [pos, mate])


def row_order():
    r = iota((64, 64), 0)
    n = iota((64, 64), 1)
    k = r & 31
    i = (k >> 3) + 4 * (k & 7)
    return jnp.where(n == jnp.where(r >= 32, 63 - i, i), 1.0, 0.0).astype(F32)


def sweep_start(gram):
    order = row_order()
    state = jnp.concatenate([dot(order, gram), order], axis=1)
    lane = iota((8, 128), 1)
    sub = iota((8, 128), 0)
    p = [state[8 * v:8 * v + 8] for v in range(4)]
    q = [state[32 + 8 * v:40 + 8 * v] for v in range(4)]
    rq = [63 - (v + 4 * sub) for v in range(4)]
    dp = [lane_gather(p[v], v + 4 * sub) for v in range(4)]
    dq = [lane_gather(q[v], rq[v]) for v in range(4)]
    mate = jnp.where(lane >= 63, 63, 63 - lane)
    return tuple(p + q + dp + dq + rq + [lane, mate])


def sweep_end(carry):
    return dot_tn(row_order(), jnp.concatenate(carry[:8], axis=0))


def split(x):
    hi = x.astype(BF16)
    return hi, (x - hi.astype(F32)).astype(BF16)


def gram_of(ah, al, bh, bl):
    dims = (((1,), (1,)), ((), ()))
    out = lax.dot_general(ah, bh, dims, preferred_element_type=F32)
    out += lax.dot_general(ah, bl, dims, preferred_element_type=F32)
    return out + lax.dot_general(al, bh, dims, preferred_element_type=F32)


def pack(g):
    return jnp.concatenate([g[:32], g[32:]], axis=1)


def unpack(p):
    return jnp.concatenate([p[:, :64], p[:, 64:]], axis=0)


def sum_chips(chips):
    return ((chips[0] + chips[1]) + (chips[2] + chips[3])) + ((chips[4] + chips[5]) + (chips[6] + chips[7]))


def front_kernel(x_ref, gt_ref, hi_out, lo_out, part, mate, chips, part2, mate2, chips2,
                 xs, hi, lo, pay, came, send_sem, recv_sem, out_sem):
    pair = lax.axis_index("pair")
    row = lax.axis_index("row")
    z = row // 2
    core = row % 2
    partner = (pair, 2 * z + (1 - core))
    others = [(pair, 2 * ((z + d) % 8) + core) for d in range(1, 8)]
    ahead = ((pair + 1) % 32, row)
    behind = ((pair + 31) % 32, row)

    def send(src, dst, slot, device):
        return pltpu.make_async_remote_copy(
            src_ref=src, dst_ref=dst, send_sem=send_sem.at[slot], recv_sem=recv_sem.at[slot],
            device_id=device, device_id_type=MESH)

    barrier = pltpu.get_barrier_semaphore()
    for device in [ahead, behind, partner] + others:
        pl.semaphore_signal(barrier, inc=1, device_id=device, device_id_type=MESH)
    x = x_ref[...]
    xh, xl = split(x)
    part[...] = pack(gram_of(xh, xl, xh, xl))
    pl.semaphore_wait(barrier, 10)

    to_mate = send(part, mate, 0, partner)
    to_mate.start()
    forward = send(x_ref, xs.at[0:64], 16, ahead)
    backward = send(x_ref, xs.at[64:128], 17, behind)
    forward.start()
    backward.start()
    to_mate.wait()
    chips[z] = part[...] + mate[...]
    copies = [send(chips.at[z], chips.at[z], d, others[d - 1]) for d in range(1, 8)]
    for copy in copies:
        copy.start()
    for copy in copies:
        copy.wait()
    carry = sweep_start(unpack(sum_chips(chips)))
    carry = lax.fori_loop(0, BREAK_1, step, carry)

    forward.wait()
    backward.wait()

    @pl.when(pair == 0)
    def _():
        xs[0:64] = x_ref[...]

    @pl.when(pair == 31)
    def _():
        xs[64:128] = x_ref[...]

    ah, al = split(xs[0:64])
    bh, bl = split(xs[64:128])
    part2[...] = pack(gram_of(ah, al, bh, bl))
    to_mate2 = send(part2, mate2, 8, partner)
    to_mate2.start()
    hi[0:64] = ah
    hi[64:128] = bh
    lo[0:64] = al
    lo[64:128] = bl
    hi_copy = pltpu.make_async_copy(hi, hi_out, out_sem.at[0])
    lo_copy = pltpu.make_async_copy(lo, lo_out, out_sem.at[1])
    hi_copy.start()
    lo_copy.start()
    carry = lax.fori_loop(BREAK_1, BREAK_2, step, carry)

    to_mate2.wait()
    chips2[z] = part2[...] + mate2[...]
    copies2 = [send(chips2.at[z], chips2.at[z], 8 + d, others[d - 1]) for d in range(1, 8)]
    for copy in copies2:
        copy.start()
    carry = lax.fori_loop(BREAK_2, STEPS, step, carry)

    done = sweep_end(carry)
    upper = done[0:32]
    lower = done[32:64]
    pay[0] = jnp.where(pair == 0, lower, upper)
    pay[1] = lower
    t_forward = send(pay.at[0], came.at[0], 18, ahead)
    t_backward = send(pay.at[1], came.at[1], 19, behind)
    t_forward.start()
    t_backward.start()
    for copy in copies2:
        copy.wait()
    cross = unpack(sum_chips(chips2))
    t_forward.wait()
    t_backward.wait()
    a = jnp.where(pair == 0, upper, came[0])
    b = jnp.where(pair == 31, upper, came[1])
    ta = a[:, 64:128]
    tb = b[:, 64:128]
    off = dot_nt(dot(ta, cross), tb)
    da = jnp.where(pair == 1, a[:, 32:64], a[:, 0:32])
    db = jnp.where(pair == 31, b[:, 0:32], b[:, 32:64])
    top = jnp.concatenate([da, off, ta], axis=1)
    bottom = jnp.concatenate([off.T, db, tb], axis=1)
    gt_ref[...] = jnp.concatenate([top, bottom], axis=0)
    hi_copy.wait()
    lo_copy.wait()


def front(matrix):
    vmem = pl.BlockSpec(memory_space=pltpu.VMEM)
    any_space = pl.BlockSpec(memory_space=pl.ANY)
    small = pltpu.VMEM((32, 128), F32)
    many = pltpu.VMEM((8, 32, 128), F32)
    return pl.pallas_call(
        front_kernel,
        out_shape=(
            jax.ShapeDtypeStruct((64, 128), F32),
            jax.ShapeDtypeStruct((128, 2048), BF16),
            jax.ShapeDtypeStruct((128, 2048), BF16),
        ),
        in_specs=[vmem],
        out_specs=(vmem, any_space, any_space),
        scratch_shapes=[
            small, small, many, small, small, many,
            pltpu.VMEM((128, 2048), F32),
            pltpu.VMEM((128, 2048), BF16),
            pltpu.VMEM((128, 2048), BF16),
            pltpu.VMEM((2, 32, 128), F32),
            pltpu.VMEM((2, 32, 128), F32),
            pltpu.SemaphoreType.DMA((20,)),
            pltpu.SemaphoreType.DMA((20,)),
            pltpu.SemaphoreType.DMA((2,)),
        ],
        compiler_params=pltpu.CompilerParams(collective_id=0, has_side_effects=True),
    )(matrix)


def back_kernel(gt_ref, hi_in, lo_in, out_ref, acc_ref, hi, lo, sem):
    hi_copy = pltpu.make_async_copy(hi_in, hi, sem.at[0])
    lo_copy = pltpu.make_async_copy(lo_in, lo, sem.at[1])
    hi_copy.start()
    lo_copy.start()
    pair = lax.axis_index("pair")
    row = lax.axis_index("row")
    carry = sweep_start(gt_ref[:, 0:64])
    carry = lax.fori_loop(0, STEPS, step, carry)
    turn = sweep_end(carry)[:, 64:128]
    qa = dot(turn[:, 0:32], gt_ref[0:32, 64:128])
    qb = dot(turn[:, 32:64], gt_ref[32:64, 64:128])
    slot_a = jnp.maximum(pair - 1, 0)
    slot_b = jnp.minimum(pair + 1, 31)
    zero = jnp.zeros((64, 64), F32)
    halves = []
    for n in range(2):
        slot = 2 * row + n
        halves.append(jnp.where(slot == slot_a, qa, jnp.where(slot == slot_b, qb, zero)))
    acc_ref[...] = jnp.concatenate(halves, axis=1)
    qh, ql = split(jnp.concatenate([qa, qb], axis=1))
    hi_copy.wait()
    lo_copy.wait()
    h = hi[...]
    out = jnp.dot(qh, h, preferred_element_type=F32)
    out += jnp.dot(ql, h, preferred_element_type=F32)
    out_ref[...] = out + jnp.dot(qh, lo[...], preferred_element_type=F32)


def back(gt, hi, lo):
    vmem = pl.BlockSpec(memory_space=pltpu.VMEM)
    any_space = pl.BlockSpec(memory_space=pl.ANY)
    return pl.pallas_call(
        back_kernel,
        out_shape=(
            jax.ShapeDtypeStruct((64, 2048), F32),
            jax.ShapeDtypeStruct((64, 128), F32),
        ),
        in_specs=[vmem, any_space, any_space],
        out_specs=(vmem, vmem),
        scratch_shapes=[
            pltpu.VMEM((128, 2048), BF16),
            pltpu.VMEM((128, 2048), BF16),
            pltpu.SemaphoreType.DMA((2,)),
        ],
    )(gt, hi, lo)


def local(matrix):
    gt, hi, lo = front(matrix)
    return back(gt, hi, lo)


def solution(mesh):
    in_specs = (P("pair", "row"),)
    out_specs = (P("pair", "row"), P("pair", "row"))
    return jax.shard_map(local, mesh=mesh, in_specs=in_specs, out_specs=out_specs, check_vma=False)
```

```python
import jax
import jax.numpy as jnp
from jax import lax
from jax.experimental import pallas as pl
from jax.experimental.pallas import tpu as pltpu
from jax.sharding import PartitionSpec as P

F32 = jnp.float32
BF16 = jnp.bfloat16
HIGH = lax.Precision.HIGHEST
MESH = pl.DeviceIdType.MESH
DOUBLES = 31
CHUNKS = 4
CHUNK = 2048 // CHUNKS
BREAKS = (0, 1, 5, 14, 23)
BREAK_2 = 29
LIMIT = 16 * 1024 * 1024
FAR_FIRST = (4, 3, 5, 2, 6, 1, 7)


def iota(shape, d):
    return lax.broadcasted_iota(jnp.int32, shape, d)


def lane_gather(x, idx):
    dims = lax.GatherDimensionNumbers(
        offset_dims=(), collapsed_slice_dims=(1,), start_index_map=(1,),
        operand_batching_dims=(0,), start_indices_batching_dims=(0,))
    return lax.gather(x, idx[..., None], dims, (1, 1), mode=lax.GatherScatterMode.PROMISE_IN_BOUNDS)


def dot(a, b):
    return jnp.dot(a, b, precision=HIGH, preferred_element_type=F32)


def dot_tn(a, b):
    return lax.dot_general(a, b, (((0,), (0,)), ((), ())), precision=HIGH, preferred_element_type=F32)


def dot_nt(a, b):
    return lax.dot_general(a, b, (((1,), (1,)), ((), ())), precision=HIGH, preferred_element_type=F32)


def angle(gpp, gqq, gpq):
    d = gqq - gpp
    ad = jnp.abs(d)
    small = jnp.maximum(ad, jnp.abs(gpq)) < 1e-15
    k = jnp.where(small, F32(2.0 ** 100), F32(1.0))
    ad = ad * k
    g = gpq * k
    b = g + g
    h = ad * ad + b * b
    r = h * lax.rsqrt(h)
    hu = 0.5 * (ad + r)
    w = lax.rsqrt(r * hu)
    c = hu * w
    s = g * jnp.where(d >= 0, w, -w)
    return c, s, s * (r * w) * gpq


def ssum(x):
    x = x + pltpu.roll(x, 4, 0)
    x = x + pltpu.roll(x, 2, 0)
    return x + pltpu.roll(x, 1, 0)


def shift(p, q, first, last):
    up = pltpu.roll(p[0], 7, 0)
    down = pltpu.roll(q[3], 1, 0)
    new_p = [jnp.where(first, p[0], p[1]), p[2], p[3], jnp.where(last, q[3], up)]
    new_q = [jnp.where(first, p[1], down), q[0], q[1], q[2]]
    return new_p, new_q


def step(_, carry):
    lane = iota((8, 128), 1)
    sub = iota((8, 128), 0)
    first, last = sub == 0, sub == 7
    wide = lane >= 64
    p, q, dp, dq, rq = [list(carry[4 * n:4 * n + 4]) for n in range(5)]
    pos, mate = carry[20], carry[21]
    near = jnp.where(wide, 127, jnp.minimum(pos, 63 - pos))
    sign = jnp.where(pos < 32, -1.0, 1.0).astype(F32)
    partner = jnp.where(mate == lane, 0, mate)
    partner = jnp.where(wide, lane, partner)
    c, s, cs, ss = [], [], [], []
    for v in range(4):
        cv, sv, fix = angle(dp[v], dq[v], lane_gather(p[v], rq[v]))
        dp[v] = dp[v] - fix
        dq[v] = dq[v] + fix
        hit = near == v + 4 * sub
        c.append(cv)
        s.append(sv)
        cs.append(jnp.where(hit, cv, 0.0))
        ss.append(jnp.where(hit, sv, 0.0))
    cc = ssum((cs[0] + cs[1]) + (cs[2] + cs[3])) + jnp.where(wide, 1.0, 0.0)
    sc = ssum((ss[0] + ss[1]) + (ss[2] + ss[3])) * sign
    for v in range(4):
        pm = lane_gather(p[v], partner)
        qm = lane_gather(q[v], partner)
        a, b = p[v], q[v]
        p[v] = (c[v] * a - s[v] * b) * cc + (c[v] * pm - s[v] * qm) * sc
        q[v] = (s[v] * a + c[v] * b) * cc + (s[v] * pm + c[v] * qm) * sc
    p, q = shift(p, q, first, last)
    dp, dq = shift(dp, dq, first, last)
    rq = [jnp.where(x == 63, 1, x + 1) for x in rq]
    pos = jnp.where(pos == 0, 0, jnp.where(pos == 1, 63, pos - 1))
    mate = mate + jnp.where(lane == 0, 1, 2)
    mate = jnp.where(mate > 63, mate - 63, mate)
    return tuple(p + q + dp + dq + rq + [pos, mate])


def row_order():
    r = iota((64, 64), 0)
    n = iota((64, 64), 1)
    k = r & 31
    i = (k >> 3) + 4 * (k & 7)
    return jnp.where(n == jnp.where(r >= 32, 63 - i, i), 1.0, 0.0).astype(F32)


def sweep_start(state):
    lane = iota((8, 128), 1)
    sub = iota((8, 128), 0)
    p = [state[8 * v:8 * v + 8] for v in range(4)]
    q = [state[32 + 8 * v:40 + 8 * v] for v in range(4)]
    rq = [63 - (v + 4 * sub) for v in range(4)]
    dp = [lane_gather(p[v], v + 4 * sub) for v in range(4)]
    dq = [lane_gather(q[v], rq[v]) for v in range(4)]
    mate = jnp.where(lane >= 63, 63, 63 - lane)
    carry = step(0, tuple(p + q + dp + dq + rq + [lane, mate]))
    return carry + (jnp.full((8, 128), 65, jnp.int32),)


def wrap(x):
    return jnp.where(x > 63, x - 63, x)


def spread(near, values, sub):
    hits = [jnp.where(near == v + 4 * sub, values[v], 0.0) for v in range(4)]
    return ssum((hits[0] + hits[1]) + (hits[2] + hits[3]))


def coefs(pos, c, s, sub, wide):
    near = jnp.where(wide, 127, jnp.minimum(pos, 63 - pos))
    sign = jnp.where(pos < 32, -1.0, 1.0).astype(F32)
    return spread(near, c, sub) + jnp.where(wide, 1.0, 0.0), spread(near, s, sub) * sign


def next_pos(pos):
    return jnp.where(pos == 0, 0, jnp.where(pos == 1, 63, pos - 1))


def partner_of(mate, lane, wide):
    return jnp.where(wide, lane, jnp.where(mate == lane, 0, mate))


def turn_rows(p, q, c, s):
    a = [c[v] * p[v] - s[v] * q[v] for v in range(4)]
    b = [s[v] * p[v] + c[v] * q[v] for v in range(4)]
    return a, b


def blend(rows, others, cc, sc):
    return [x * cc + y * sc for x, y in zip(rows, others)]


def double_step(_, carry):
    lane = iota((8, 128), 1)
    sub = iota((8, 128), 0)
    first, last = sub == 0, sub == 7
    wide = lane >= 64
    p, q, dp, dq, rq = [list(carry[4 * n:4 * n + 4]) for n in range(5)]
    pos, mate, twice = carry[20], carry[21], carry[22]
    pos2 = next_pos(pos)
    mate2 = wrap(mate + jnp.where(lane == 0, 1, 2))
    one = partner_of(mate, lane, wide)
    two = partner_of(mate2, lane, wide)
    both = lane_gather(one, two)

    g = [lane_gather(p[v], rq[v]) for v in range(4)]
    pz, qz = list(p), list(q)
    pz[1] = jnp.where(first, pltpu.roll(q[3], 1, 0), p[1])
    qz[1] = jnp.where(first, pltpu.roll(p[3], 1, 0), q[1])
    ra, rb = [], []
    for v in range(4):
        step_by = 2
        if v == 0:
            step_by = jnp.where(first, 1, 2)
        if v == 1:
            step_by = jnp.where(first, 34, 2)
        n = wrap(rq[v] + step_by)
        m = wrap(twice - n)
        m = jnp.where(m == n, 0, m)
        ra.append((lane_gather(pz[v], n), lane_gather(qz[v], n)))
        rb.append((lane_gather(pz[v], m), lane_gather(qz[v], m)))
    pa = [lane_gather(x, one) for x in p]
    qa = [lane_gather(x, one) for x in q]
    pb = [lane_gather(x, two) for x in p]
    qb = [lane_gather(x, two) for x in q]
    pc = [lane_gather(x, both) for x in p]
    qc = [lane_gather(x, both) for x in q]

    c, s = [], []
    for v in range(4):
        cv, sv, fix = angle(dp[v], dq[v], g[v])
        dp[v] = dp[v] - fix
        dq[v] = dq[v] + fix
        c.append(cv)
        s.append(sv)
    dp, dq = shift(dp, dq, first, last)

    c2r, c3r = pltpu.roll(c[2], 1, 0), pltpu.roll(c[3], 1, 0)
    s2r, s3r = pltpu.roll(s[2], 1, 0), pltpu.roll(s[3], 1, 0)
    cz = [c[0], jnp.where(first, c3r, c[1]), c[2], c[3]]
    sz = [s[0], jnp.where(first, -s3r, s[1]), s[2], s[3]]
    cn = [jnp.where(first, c[1], c2r), jnp.where(first, c2r, c3r), c[0], c[1]]
    sn = [jnp.where(first, -s[1], s2r), jnp.where(first, s2r, s3r), s[0], s[1]]
    gs = []
    for v in range(4):
        at_n = cz[v] * ra[v][0] - sz[v] * ra[v][1]
        at_m = cz[v] * rb[v][0] - sz[v] * rb[v][1]
        gs.append(at_n * cn[v] + at_m * sn[v])
    g2 = [jnp.where(first, gs[0], gs[1]), gs[2], gs[3],
          jnp.where(last, pltpu.roll(gs[1], 7, 0), pltpu.roll(gs[0], 7, 0))]
    c2, s2 = [], []
    for v in range(4):
        cv, sv, fix = angle(dp[v], dq[v], g2[v])
        dp[v] = dp[v] - fix
        dq[v] = dq[v] + fix
        c2.append(cv)
        s2.append(sv)
    dp, dq = shift(dp, dq, first, last)

    cc, sc = coefs(pos, c, s, sub, wide)
    far = 63 - pos2
    far = jnp.where(far == 0, 0, jnp.where(far == 63, 1, far + 1))
    ccp, scp = coefs(far, c, s, sub, wide)
    p1, q1 = turn_rows(p, q, c, s)
    p1a, q1a = turn_rows(pa, qa, c, s)
    p1b, q1b = turn_rows(pb, qb, c, s)
    p1c, q1c = turn_rows(pc, qc, c, s)
    p, q = shift(blend(p1, p1a, cc, sc), blend(q1, q1a, cc, sc), first, last)
    pm, qm = shift(blend(p1b, p1c, ccp, scp), blend(q1b, q1c, ccp, scp), first, last)
    cc2, sc2 = coefs(pos2, c2, s2, sub, wide)
    p2, q2 = turn_rows(p, q, c2, s2)
    p2m, q2m = turn_rows(pm, qm, c2, s2)
    p, q = shift(blend(p2, p2m, cc2, sc2), blend(q2, q2m, cc2, sc2), first, last)
    rq = [wrap(wrap(x + 1) + 1) for x in rq]
    mate = wrap(mate2 + jnp.where(lane == 0, 1, 2))
    twice = jnp.where(twice + 4 > 126, twice - 59, twice + 4)
    return tuple(p + q + dp + dq + rq + [next_pos(pos2), mate, twice])


def split(x):
    hi = x.astype(BF16)
    return hi, (x - hi.astype(F32)).astype(BF16)


def gram_of(ah, al, bh, bl):
    dims = (((1,), (1,)), ((), ()))
    out = lax.dot_general(ah, bh, dims, preferred_element_type=F32)
    out += lax.dot_general(ah, bl, dims, preferred_element_type=F32)
    return out + lax.dot_general(al, bh, dims, preferred_element_type=F32)


def product(ah, al, bh, bl):
    out = jnp.dot(ah, bh, preferred_element_type=F32)
    out += jnp.dot(ah, bl, preferred_element_type=F32)
    return out + jnp.dot(al, bh, preferred_element_type=F32)


def pack(g):
    return jnp.concatenate([g[:32], g[32:]], axis=1)


def unpack(p):
    return jnp.concatenate([p[:, :64], p[:, 64:]], axis=0)


def sum_chips(chips):
    return ((chips[0] + chips[1]) + (chips[2] + chips[3])) + ((chips[4] + chips[5]) + (chips[6] + chips[7]))


def front_kernel(x_in, gt_ref, yh_ref, yl_ref, x_ref, part, mate, chips, part2, mate2, chips2,
                 xs, hi, lo, pay, came, send_sem, recv_sem, local_sem):
    pair = lax.axis_index("pair")
    row = lax.axis_index("row")
    z = row // 2
    core = row % 2
    partner = (pair, 2 * z + (1 - core))
    others = [(pair, 2 * ((z + d) % 8) + core) for d in FAR_FIRST]
    ahead = ((pair + 1) % 32, row)
    behind = ((pair + 31) % 32, row)
    has_ahead = pair < 31
    has_behind = pair > 0

    def send(src, dst, slot, device):
        return pltpu.make_async_remote_copy(
            src_ref=src, dst_ref=dst, send_sem=send_sem.at[slot], recv_sem=recv_sem.at[slot],
            device_id=device, device_id_type=MESH)

    def start_both(forward, backward):
        pl.when(has_ahead)(forward.start)
        pl.when(has_behind)(backward.start)

    def wait_both(forward, backward):
        pl.when(has_behind)(forward.wait_recv)
        pl.when(has_ahead)(backward.wait_recv)
        pl.when(has_ahead)(forward.wait_send)
        pl.when(has_behind)(backward.wait_send)

    load = pltpu.make_async_copy(x_in, x_ref, local_sem)
    load.start()
    barrier = pltpu.get_barrier_semaphore()

    def greet(device):
        pl.semaphore_signal(barrier, inc=1, device_id=device, device_id_type=MESH)

    pl.when(has_ahead)(lambda: greet(ahead))
    pl.when(has_behind)(lambda: greet(behind))
    for device in others + [partner]:
        greet(device)
    pl.semaphore_wait(barrier, 8 + jnp.where(has_ahead, 1, 0) + jnp.where(has_behind, 1, 0))

    blocks = []
    for n in range(CHUNKS):
        lanes = pl.ds(n * CHUNK, CHUNK)
        forward = send(x_in.at[:, lanes], xs.at[0:64, lanes], 18 + 2 * n, ahead)
        backward = send(x_in.at[:, lanes], xs.at[64:128, lanes], 19 + 2 * n, behind)
        start_both(forward, backward)
        blocks.append((forward, backward))
    load.wait()
    xh, xl = split(x_ref[...])
    part[...] = pack(gram_of(xh, xl, xh, xl))
    to_mate = send(part, mate, 0, partner)
    to_mate.start()
    to_mate.wait()
    chips[z] = part[...] + mate[...]
    copies = [send(chips.at[z], chips.at[z], 1 + n, device) for n, device in enumerate(others)]
    for copy in copies:
        copy.start()
    for copy in copies:
        copy.wait()
    order = row_order()
    gram = unpack(sum_chips(chips))
    carry = sweep_start(jnp.concatenate([dot(order, gram), order], axis=1))

    cross = jnp.zeros((64, 64), F32)
    for n, (forward, backward) in enumerate(blocks):
        carry = lax.fori_loop(BREAKS[n], BREAKS[n + 1], double_step, carry)
        wait_both(forward, backward)
        lanes = pl.ds(n * CHUNK, CHUNK)

        @pl.when(pair == 0)
        def _():
            xs[0:64, lanes] = x_ref[:, lanes]

        @pl.when(pair == 31)
        def _():
            xs[64:128, lanes] = x_ref[:, lanes]

        ah, al = split(xs[0:64, lanes])
        bh, bl = split(xs[64:128, lanes])
        cross += gram_of(ah, al, bh, bl)
        hi[0:64, lanes] = ah
        hi[64:128, lanes] = bh
        lo[0:64, lanes] = al
        lo[64:128, lanes] = bl
    part2[...] = pack(cross)
    to_mate2 = send(part2, mate2, 8, partner)
    to_mate2.start()
    carry = lax.fori_loop(BREAKS[CHUNKS], BREAK_2, double_step, carry)
    to_mate2.wait()
    chips2[z] = part2[...] + mate2[...]
    copies2 = [send(chips2.at[z], chips2.at[z], 9 + n, device) for n, device in enumerate(others)]
    for copy in copies2:
        copy.start()
    carry = lax.fori_loop(BREAK_2, DOUBLES, double_step, carry)

    upper = jnp.concatenate(carry[0:4], axis=0)
    lower = jnp.concatenate(carry[4:8], axis=0)
    top_order = order[0:32, 0:32]
    bottom_order = order[32:64, 32:64]
    flip = dot_nt(top_order, bottom_order)
    pay[0] = jnp.where(pair == 0, dot(flip, lower), upper)
    pay[1] = lower
    t_forward = send(pay.at[0], came.at[0], 16, ahead)
    t_backward = send(pay.at[1], came.at[1], 17, behind)
    start_both(t_forward, t_backward)
    turned = dot(flip, upper)
    wait_both(t_forward, t_backward)
    a = jnp.where(pair == 0, upper, came[0])
    b = jnp.where(pair == 31, turned, came[1])
    ta = a[:, 64:128]
    tb = b[:, 64:128]
    ta_flat = dot_tn(top_order, ta)
    tb_flat = dot_tn(bottom_order, tb)
    da = jnp.where(pair == 1, a[:, 32:64], a[:, 0:32])
    db = jnp.where(pair == 31, b[:, 0:32], b[:, 32:64])
    tah, tal = split(ta_flat)
    tbh, tbl = split(tb_flat)
    for n in range(CHUNKS):
        lanes = pl.ds(n * CHUNK, CHUNK)
        yh_ref[0:32, lanes], yl_ref[0:32, lanes] = split(product(tah, tal, hi[0:64, lanes], lo[0:64, lanes]))
        yh_ref[32:64, lanes], yl_ref[32:64, lanes] = split(product(tbh, tbl, hi[64:128, lanes], lo[64:128, lanes]))
    for copy in copies2:
        copy.wait()
    cross = unpack(sum_chips(chips2))
    off = dot_nt(dot(ta, cross), tb_flat)
    off_t = dot_nt(dot_nt(tb, cross), ta_flat)
    gt_ref[0:32] = jnp.concatenate([da, off, ta_flat], axis=1)
    gt_ref[32:64] = jnp.concatenate([off_t, db, tb_flat], axis=1)


def front(matrix):
    vmem = pl.BlockSpec(memory_space=pltpu.VMEM)
    small = pltpu.VMEM((32, 128), F32)
    many = pltpu.VMEM((8, 32, 128), F32)
    return pl.pallas_call(
        front_kernel,
        out_shape=(
            jax.ShapeDtypeStruct((64, 128), F32),
            jax.ShapeDtypeStruct((64, 2048), BF16),
            jax.ShapeDtypeStruct((64, 2048), BF16),
        ),
        in_specs=[pl.BlockSpec(memory_space=pltpu.HBM)],
        out_specs=(vmem, vmem, vmem),
        scratch_shapes=[
            pltpu.VMEM((64, 2048), F32),
            small, small, many, small, small, many,
            pltpu.VMEM((128, 2048), F32),
            pltpu.VMEM((128, 2048), BF16),
            pltpu.VMEM((128, 2048), BF16),
            pltpu.VMEM((2, 32, 128), F32),
            pltpu.VMEM((2, 32, 128), F32),
            pltpu.SemaphoreType.DMA((18 + 2 * CHUNKS,)),
            pltpu.SemaphoreType.DMA((18 + 2 * CHUNKS,)),
            pltpu.SemaphoreType.DMA(()),
        ],
        compiler_params=pltpu.CompilerParams(
            collective_id=0, has_side_effects=True, vmem_limit_bytes=LIMIT),
    )(matrix)


def back_kernel(gt_ref, yh_ref, yl_ref, out_ref, acc_ref):
    pair = lax.axis_index("pair")
    row = lax.axis_index("row")
    order = row_order()
    carry = sweep_start(jnp.concatenate([gt_ref[:, 0:64], order], axis=1))
    carry = lax.fori_loop(0, DOUBLES, double_step, carry)
    vh, vl = split(jnp.concatenate(carry[0:8], axis=0)[:, 64:128])
    unorder = order.astype(BF16)
    dims = (((0,), (0,)), ((), ()))
    th = lax.dot_general(unorder, vh, dims, preferred_element_type=F32)
    tl = lax.dot_general(unorder, vl, dims, preferred_element_type=F32)
    out_ref[...] = product(th.astype(BF16), tl.astype(BF16), yh_ref[...], yl_ref[...])
    turn = th + tl
    qa = dot(turn[:, 0:32], gt_ref[0:32, 64:128])
    qb = dot(turn[:, 32:64], gt_ref[32:64, 64:128])
    slot_a = jnp.maximum(pair - 1, 0)
    slot_b = jnp.minimum(pair + 1, 31)
    zero = jnp.zeros((64, 64), F32)
    halves = []
    for n in range(2):
        slot = 2 * row + n
        halves.append(jnp.where(slot == slot_a, qa, jnp.where(slot == slot_b, qb, zero)))
    acc_ref[...] = jnp.concatenate(halves, axis=1)


def back(gt, yh, yl):
    vmem = pl.BlockSpec(memory_space=pltpu.VMEM)
    return pl.pallas_call(
        back_kernel,
        out_shape=(
            jax.ShapeDtypeStruct((64, 2048), F32),
            jax.ShapeDtypeStruct((64, 128), F32),
        ),
        in_specs=[vmem, vmem, vmem],
        out_specs=(vmem, vmem),
        compiler_params=pltpu.CompilerParams(vmem_limit_bytes=LIMIT),
    )(gt, yh, yl)


def local(matrix):
    gt, yh, yl = front(pltpu.with_memory_space_constraint(matrix, pltpu.HBM))
    return back(gt, yh, yl)


def solution(mesh):
    in_specs = (P("pair", "row"),)
    out_specs = (P("pair", "row"), P("pair", "row"))
    return jax.shard_map(local, mesh=mesh, in_specs=in_specs, out_specs=out_specs, check_vma=False)
```

```python
import jax
import jax.numpy as jnp
from jax import lax
from jax.experimental import pallas as pl
from jax.experimental.pallas import tpu as pltpu
from jax.sharding import PartitionSpec as P

F32 = jnp.float32
BF16 = jnp.bfloat16
HIGH = lax.Precision.HIGHEST
MESH = pl.DeviceIdType.MESH
DOUBLES = 31
CHUNKS = 4
CHUNK = 2048 // CHUNKS
EARLY = 1
BREAKS = (0, 0, 1, 8, 16)
BREAK_2 = 25
LIMIT = 16 * 1024 * 1024
FAR_FIRST = (4, 3, 5, 2, 6, 1, 7)


def iota(shape, d):
    return lax.broadcasted_iota(jnp.int32, shape, d)


def lane_gather(x, idx):
    dims = lax.GatherDimensionNumbers(
        offset_dims=(), collapsed_slice_dims=(1,), start_index_map=(1,),
        operand_batching_dims=(0,), start_indices_batching_dims=(0,))
    return lax.gather(x, idx[..., None], dims, (1, 1), mode=lax.GatherScatterMode.PROMISE_IN_BOUNDS)


def dot(a, b):
    return jnp.dot(a, b, precision=HIGH, preferred_element_type=F32)


def dot_tn(a, b):
    return lax.dot_general(a, b, (((0,), (0,)), ((), ())), precision=HIGH, preferred_element_type=F32)


def dot_nt(a, b):
    return lax.dot_general(a, b, (((1,), (1,)), ((), ())), precision=HIGH, preferred_element_type=F32)


def angle(gpp, gqq, gpq):
    d = gqq - gpp
    ad = jnp.abs(d)
    small = jnp.maximum(ad, jnp.abs(gpq)) < 1e-15
    k = jnp.where(small, F32(2.0 ** 100), F32(1.0))
    ad = ad * k
    g = gpq * k
    b = g + g
    h = ad * ad + b * b
    r = h * lax.rsqrt(h)
    hu = 0.5 * (ad + r)
    w = lax.rsqrt(r * hu)
    c = hu * w
    s = g * jnp.where(d >= 0, w, -w)
    return c, s, s * (r * w) * gpq


def ssum(x):
    x = x + pltpu.roll(x, 4, 0)
    x = x + pltpu.roll(x, 2, 0)
    return x + pltpu.roll(x, 1, 0)


def shift(p, q, first, last):
    up = pltpu.roll(p[0], 7, 0)
    down = pltpu.roll(q[3], 1, 0)
    new_p = [jnp.where(first, p[0], p[1]), p[2], p[3], jnp.where(last, q[3], up)]
    new_q = [jnp.where(first, p[1], down), q[0], q[1], q[2]]
    return new_p, new_q


def step(_, carry):
    lane = iota((8, 128), 1)
    sub = iota((8, 128), 0)
    first, last = sub == 0, sub == 7
    wide = lane >= 64
    p, q, dp, dq, rq = [list(carry[4 * n:4 * n + 4]) for n in range(5)]
    pos, mate = carry[20], carry[21]
    near = jnp.where(wide, 127, jnp.minimum(pos, 63 - pos))
    sign = jnp.where(pos < 32, -1.0, 1.0).astype(F32)
    partner = jnp.where(mate == lane, 0, mate)
    partner = jnp.where(wide, lane, partner)
    c, s, cs, ss = [], [], [], []
    for v in range(4):
        cv, sv, fix = angle(dp[v], dq[v], lane_gather(p[v], rq[v]))
        dp[v] = dp[v] - fix
        dq[v] = dq[v] + fix
        hit = near == v + 4 * sub
        c.append(cv)
        s.append(sv)
        cs.append(jnp.where(hit, cv, 0.0))
        ss.append(jnp.where(hit, sv, 0.0))
    cc = ssum((cs[0] + cs[1]) + (cs[2] + cs[3])) + jnp.where(wide, 1.0, 0.0)
    sc = ssum((ss[0] + ss[1]) + (ss[2] + ss[3])) * sign
    for v in range(4):
        pm = lane_gather(p[v], partner)
        qm = lane_gather(q[v], partner)
        a, b = p[v], q[v]
        p[v] = (c[v] * a - s[v] * b) * cc + (c[v] * pm - s[v] * qm) * sc
        q[v] = (s[v] * a + c[v] * b) * cc + (s[v] * pm + c[v] * qm) * sc
    p, q = shift(p, q, first, last)
    dp, dq = shift(dp, dq, first, last)
    rq = [jnp.where(x == 63, 1, x + 1) for x in rq]
    pos = jnp.where(pos == 0, 0, jnp.where(pos == 1, 63, pos - 1))
    mate = mate + jnp.where(lane == 0, 1, 2)
    mate = jnp.where(mate > 63, mate - 63, mate)
    return tuple(p + q + dp + dq + rq + [pos, mate])


def row_order():
    r = iota((64, 64), 0)
    n = iota((64, 64), 1)
    k = r & 31
    i = (k >> 3) + 4 * (k & 7)
    return jnp.where(n == jnp.where(r >= 32, 63 - i, i), 1.0, 0.0).astype(F32)


def sweep_start(state):
    lane = iota((8, 128), 1)
    sub = iota((8, 128), 0)
    p = [state[8 * v:8 * v + 8] for v in range(4)]
    q = [state[32 + 8 * v:40 + 8 * v] for v in range(4)]
    rq = [63 - (v + 4 * sub) for v in range(4)]
    dp = [lane_gather(p[v], v + 4 * sub) for v in range(4)]
    dq = [lane_gather(q[v], rq[v]) for v in range(4)]
    mate = jnp.where(lane >= 63, 63, 63 - lane)
    carry = step(0, tuple(p + q + dp + dq + rq + [lane, mate]))
    return carry + (jnp.full((8, 128), 65, jnp.int32),)


def wrap(x):
    return jnp.where(x > 63, x - 63, x)


def spread(near, values, sub):
    hits = [jnp.where(near == v + 4 * sub, values[v], 0.0) for v in range(4)]
    return ssum((hits[0] + hits[1]) + (hits[2] + hits[3]))


def coefs(pos, c, s, sub, wide):
    near = jnp.where(wide, 127, jnp.minimum(pos, 63 - pos))
    sign = jnp.where(pos < 32, -1.0, 1.0).astype(F32)
    return spread(near, c, sub) + jnp.where(wide, 1.0, 0.0), spread(near, s, sub) * sign


def next_pos(pos):
    return jnp.where(pos == 0, 0, jnp.where(pos == 1, 63, pos - 1))


def partner_of(mate, lane, wide):
    return jnp.where(wide, lane, jnp.where(mate == lane, 0, mate))


def turn_rows(p, q, c, s):
    a = [c[v] * p[v] - s[v] * q[v] for v in range(4)]
    b = [s[v] * p[v] + c[v] * q[v] for v in range(4)]
    return a, b


def blend(rows, others, cc, sc):
    return [x * cc + y * sc for x, y in zip(rows, others)]


def double_step(_, carry):
    lane = iota((8, 128), 1)
    sub = iota((8, 128), 0)
    first, last = sub == 0, sub == 7
    wide = lane >= 64
    p, q, dp, dq, rq = [list(carry[4 * n:4 * n + 4]) for n in range(5)]
    pos, mate, twice = carry[20], carry[21], carry[22]
    pos2 = next_pos(pos)
    mate2 = wrap(mate + jnp.where(lane == 0, 1, 2))
    one = partner_of(mate, lane, wide)
    two = partner_of(mate2, lane, wide)
    both = lane_gather(one, two)

    g = [lane_gather(p[v], rq[v]) for v in range(4)]
    pz, qz = list(p), list(q)
    pz[1] = jnp.where(first, pltpu.roll(q[3], 1, 0), p[1])
    qz[1] = jnp.where(first, pltpu.roll(p[3], 1, 0), q[1])
    ra, rb = [], []
    for v in range(4):
        step_by = 2
        if v == 0:
            step_by = jnp.where(first, 1, 2)
        if v == 1:
            step_by = jnp.where(first, 34, 2)
        n = wrap(rq[v] + step_by)
        m = wrap(twice - n)
        m = jnp.where(m == n, 0, m)
        ra.append((lane_gather(pz[v], n), lane_gather(qz[v], n)))
        rb.append((lane_gather(pz[v], m), lane_gather(qz[v], m)))
    pa = [lane_gather(x, one) for x in p]
    qa = [lane_gather(x, one) for x in q]
    pb = [lane_gather(x, two) for x in p]
    qb = [lane_gather(x, two) for x in q]
    pc = [lane_gather(x, both) for x in p]
    qc = [lane_gather(x, both) for x in q]

    c, s = [], []
    for v in range(4):
        cv, sv, fix = angle(dp[v], dq[v], g[v])
        dp[v] = dp[v] - fix
        dq[v] = dq[v] + fix
        c.append(cv)
        s.append(sv)
    dp, dq = shift(dp, dq, first, last)

    c2r, c3r = pltpu.roll(c[2], 1, 0), pltpu.roll(c[3], 1, 0)
    s2r, s3r = pltpu.roll(s[2], 1, 0), pltpu.roll(s[3], 1, 0)
    cz = [c[0], jnp.where(first, c3r, c[1]), c[2], c[3]]
    sz = [s[0], jnp.where(first, -s3r, s[1]), s[2], s[3]]
    cn = [jnp.where(first, c[1], c2r), jnp.where(first, c2r, c3r), c[0], c[1]]
    sn = [jnp.where(first, -s[1], s2r), jnp.where(first, s2r, s3r), s[0], s[1]]
    gs = []
    for v in range(4):
        at_n = cz[v] * ra[v][0] - sz[v] * ra[v][1]
        at_m = cz[v] * rb[v][0] - sz[v] * rb[v][1]
        gs.append(at_n * cn[v] + at_m * sn[v])
    g2 = [jnp.where(first, gs[0], gs[1]), gs[2], gs[3],
          jnp.where(last, pltpu.roll(gs[1], 7, 0), pltpu.roll(gs[0], 7, 0))]
    c2, s2 = [], []
    for v in range(4):
        cv, sv, fix = angle(dp[v], dq[v], g2[v])
        dp[v] = dp[v] - fix
        dq[v] = dq[v] + fix
        c2.append(cv)
        s2.append(sv)
    dp, dq = shift(dp, dq, first, last)

    cc, sc = coefs(pos, c, s, sub, wide)
    far = 63 - pos2
    far = jnp.where(far == 0, 0, jnp.where(far == 63, 1, far + 1))
    ccp, scp = coefs(far, c, s, sub, wide)
    p1, q1 = turn_rows(p, q, c, s)
    p1a, q1a = turn_rows(pa, qa, c, s)
    p1b, q1b = turn_rows(pb, qb, c, s)
    p1c, q1c = turn_rows(pc, qc, c, s)
    p, q = shift(blend(p1, p1a, cc, sc), blend(q1, q1a, cc, sc), first, last)
    pm, qm = shift(blend(p1b, p1c, ccp, scp), blend(q1b, q1c, ccp, scp), first, last)
    cc2, sc2 = coefs(pos2, c2, s2, sub, wide)
    p2, q2 = turn_rows(p, q, c2, s2)
    p2m, q2m = turn_rows(pm, qm, c2, s2)
    p, q = shift(blend(p2, p2m, cc2, sc2), blend(q2, q2m, cc2, sc2), first, last)
    rq = [wrap(wrap(x + 1) + 1) for x in rq]
    mate = wrap(mate2 + jnp.where(lane == 0, 1, 2))
    twice = jnp.where(twice + 4 > 126, twice - 59, twice + 4)
    return tuple(p + q + dp + dq + rq + [next_pos(pos2), mate, twice])


def split(x):
    hi = x.astype(BF16)
    return hi, (x - hi.astype(F32)).astype(BF16)


def gram_of(ah, al, bh, bl):
    dims = (((1,), (1,)), ((), ()))
    rows = ah.shape[0]
    both = lax.dot_general(jnp.concatenate([ah, al], axis=0), bh, dims, preferred_element_type=F32)
    return (both[:rows] + both[rows:]) + lax.dot_general(ah, bl, dims, preferred_element_type=F32)


def product(ah, al, bh, bl):
    rows = ah.shape[0]
    both = jnp.dot(jnp.concatenate([ah, al], axis=0), bh, preferred_element_type=F32)
    return (both[:rows] + both[rows:]) + jnp.dot(ah, bl, preferred_element_type=F32)


def pack(g):
    return jnp.concatenate([g[:32], g[32:]], axis=1)


def unpack(p):
    return jnp.concatenate([p[:, :64], p[:, 64:]], axis=0)


def sum_chips(chips):
    return ((chips[0] + chips[1]) + (chips[2] + chips[3])) + ((chips[4] + chips[5]) + (chips[6] + chips[7]))


def front_kernel(x_in, gt_ref, yh_ref, yl_ref, x_ref, part, mate, chips, part2, mate2, chips2,
                 xs, hi, lo, pay, came, send_sem, recv_sem, local_sem, up_sem, down_sem):
    pair = lax.axis_index("pair")
    row = lax.axis_index("row")
    z = row // 2
    core = row % 2
    partner = (pair, 2 * z + (1 - core))
    others = [(pair, 2 * ((z + d) % 8) + core) for d in FAR_FIRST]
    ahead = ((pair + 1) % 32, row)
    behind = ((pair + 31) % 32, row)
    has_ahead = pair < 31
    has_behind = pair > 0

    def send(src, dst, slot, device):
        return pltpu.make_async_remote_copy(
            src_ref=src, dst_ref=dst, send_sem=send_sem.at[slot], recv_sem=recv_sem.at[slot],
            device_id=device, device_id_type=MESH)

    def start_both(forward, backward):
        pl.when(has_ahead)(forward.start)
        pl.when(has_behind)(backward.start)

    def wait_both(forward, backward):
        pl.when(has_behind)(forward.wait_recv)
        pl.when(has_ahead)(backward.wait_recv)
        pl.when(has_ahead)(forward.wait_send)
        pl.when(has_behind)(backward.wait_send)

    load = pltpu.make_async_copy(x_in, x_ref, local_sem)
    load.start()
    barrier = pltpu.get_barrier_semaphore()

    def greet(device):
        pl.semaphore_signal(barrier, inc=1, device_id=device, device_id_type=MESH)

    pl.when(has_ahead)(lambda: greet(ahead))
    pl.when(has_behind)(lambda: greet(behind))
    above = (pair, 2 * ((z + 1) % 8) + core)
    below = (pair, 2 * ((z + 7) % 8) + core)
    for device in (partner, above, below):
        greet(device)
    pl.semaphore_wait(barrier, 3 + jnp.where(has_ahead, 1, 0) + jnp.where(has_behind, 1, 0))

    blocks = []
    for n in range(CHUNKS):
        lanes = pl.ds(n * CHUNK, CHUNK)
        forward = send(x_in.at[:, lanes], xs.at[0:64, lanes], 18 + 2 * n, ahead)
        backward = send(x_in.at[:, lanes], xs.at[64:128, lanes], 19 + 2 * n, behind)
        start_both(forward, backward)
        blocks.append((forward, backward))
    def tell(sem, n, device):
        pl.semaphore_signal(sem.at[n], inc=1, device_id=device, device_id_type=MESH)

    tell(up_sem, 0, above)
    tell(down_sem, 0, below)
    load.wait()
    xh, xl = split(x_ref[...])
    part[...] = pack(gram_of(xh, xl, xh, xl))
    to_mate = send(part, mate, 0, partner)
    to_mate.start()
    to_mate.wait()
    pl.semaphore_wait(up_sem.at[0], 1)
    tell(up_sem, 1, above)
    pl.semaphore_wait(down_sem.at[0], 1)
    tell(down_sem, 1, below)
    pl.semaphore_wait(up_sem.at[1], 1)
    tell(up_sem, 2, above)
    pl.semaphore_wait(down_sem.at[1], 1)
    pl.semaphore_wait(up_sem.at[2], 1)
    chips[z] = part[...] + mate[...]
    copies = [send(chips.at[z], chips.at[z], 1 + n, device) for n, device in enumerate(others)]
    for copy in copies:
        copy.start()

    def take(n, cross):
        wait_both(*blocks[n])
        lanes = pl.ds(n * CHUNK, CHUNK)

        @pl.when(pair == 0)
        def _():
            xs[0:64, lanes] = x_ref[:, lanes]

        @pl.when(pair == 31)
        def _():
            xs[64:128, lanes] = x_ref[:, lanes]

        ah, al = split(xs[0:64, lanes])
        bh, bl = split(xs[64:128, lanes])
        hi[0:64, lanes] = ah
        hi[64:128, lanes] = bh
        lo[0:64, lanes] = al
        lo[64:128, lanes] = bl
        return cross + gram_of(ah, al, bh, bl)

    cross = jnp.zeros((64, 64), F32)
    for n in range(EARLY):
        cross = take(n, cross)
    for copy in copies:
        copy.wait()
    order = row_order()
    gram = unpack(sum_chips(chips))
    carry = sweep_start(jnp.concatenate([dot(order, gram), order], axis=1))
    for n in range(EARLY, CHUNKS):
        if BREAKS[n] < BREAKS[n + 1]:
            carry = lax.fori_loop(BREAKS[n], BREAKS[n + 1], double_step, carry)
        cross = take(n, cross)
    part2[...] = pack(cross)
    to_mate2 = send(part2, mate2, 8, partner)
    to_mate2.start()
    carry = lax.fori_loop(BREAKS[CHUNKS], BREAK_2, double_step, carry)
    to_mate2.wait()
    chips2[z] = part2[...] + mate2[...]
    copies2 = [send(chips2.at[z], chips2.at[z], 9 + n, device) for n, device in enumerate(others)]
    for copy in copies2:
        copy.start()
    carry = lax.fori_loop(BREAK_2, DOUBLES, double_step, carry)

    upper = jnp.concatenate(carry[0:4], axis=0)
    lower = jnp.concatenate(carry[4:8], axis=0)
    top_order = order[0:32, 0:32]
    bottom_order = order[32:64, 32:64]
    flip = dot_nt(top_order, bottom_order)
    pay[0] = upper
    pay[1] = lower

    @pl.when(pair == 0)
    def _():
        pay[0] = dot(flip, lower)

    t_forward = send(pay.at[0], came.at[0], 16, ahead)
    t_backward = send(pay.at[1], came.at[1], 17, behind)
    start_both(t_forward, t_backward)
    turned = dot(flip, upper)
    wait_both(t_forward, t_backward)
    a = jnp.where(pair == 0, upper, came[0])
    b = jnp.where(pair == 31, turned, came[1])
    ta = a[:, 64:128]
    tb = b[:, 64:128]
    ta_flat = dot_tn(top_order, ta)
    tb_flat = dot_tn(bottom_order, tb)
    da = jnp.where(pair == 1, a[:, 32:64], a[:, 0:32])
    db = jnp.where(pair == 31, b[:, 0:32], b[:, 32:64])
    tah, tal = split(ta_flat)
    tbh, tbl = split(tb_flat)
    for n in range(CHUNKS):
        lanes = pl.ds(n * CHUNK, CHUNK)
        yh_ref[0:32, lanes], yl_ref[0:32, lanes] = split(product(tah, tal, hi[0:64, lanes], lo[0:64, lanes]))
        yh_ref[32:64, lanes], yl_ref[32:64, lanes] = split(product(tbh, tbl, hi[64:128, lanes], lo[64:128, lanes]))
    for copy in copies2:
        copy.wait()
    cross = unpack(sum_chips(chips2))
    off = dot_nt(dot(ta, cross), tb_flat)
    off_t = dot_nt(dot_nt(tb, cross), ta_flat)
    gt_ref[0:32] = jnp.concatenate([da, off, ta_flat], axis=1)
    gt_ref[32:64] = jnp.concatenate([off_t, db, tb_flat], axis=1)


def front(matrix):
    vmem = pl.BlockSpec(memory_space=pltpu.VMEM)
    small = pltpu.VMEM((32, 128), F32)
    many = pltpu.VMEM((8, 32, 128), F32)
    return pl.pallas_call(
        front_kernel,
        out_shape=(
            jax.ShapeDtypeStruct((64, 128), F32),
            jax.ShapeDtypeStruct((64, 2048), BF16),
            jax.ShapeDtypeStruct((64, 2048), BF16),
        ),
        in_specs=[pl.BlockSpec(memory_space=pltpu.HBM)],
        out_specs=(vmem, vmem, vmem),
        scratch_shapes=[
            pltpu.VMEM((64, 2048), F32),
            small, small, many, small, small, many,
            pltpu.VMEM((128, 2048), F32),
            pltpu.VMEM((128, 2048), BF16),
            pltpu.VMEM((128, 2048), BF16),
            pltpu.VMEM((2, 32, 128), F32),
            pltpu.VMEM((2, 32, 128), F32),
            pltpu.SemaphoreType.DMA((18 + 2 * CHUNKS,)),
            pltpu.SemaphoreType.DMA((18 + 2 * CHUNKS,)),
            pltpu.SemaphoreType.DMA(()),
            pltpu.SemaphoreType.REGULAR((3,)),
            pltpu.SemaphoreType.REGULAR((2,)),
        ],
        compiler_params=pltpu.CompilerParams(
            collective_id=0, has_side_effects=True, vmem_limit_bytes=LIMIT),
    )(matrix)


def back_kernel(gt_ref, yh_ref, yl_ref, out_ref, acc_ref):
    pair = lax.axis_index("pair")
    row = lax.axis_index("row")
    order = row_order()
    carry = sweep_start(jnp.concatenate([gt_ref[:, 0:64], order], axis=1))
    carry = lax.fori_loop(0, DOUBLES, double_step, carry)
    vh, vl = split(jnp.concatenate(carry[0:8], axis=0)[:, 64:128])
    unorder = order.astype(BF16)
    dims = (((0,), (0,)), ((), ()))
    th = lax.dot_general(unorder, vh, dims, preferred_element_type=F32)
    tl = lax.dot_general(unorder, vl, dims, preferred_element_type=F32)
    out_ref[...] = product(th.astype(BF16), tl.astype(BF16), yh_ref[...], yl_ref[...])
    turn = th + tl
    qa = dot(turn[:, 0:32], gt_ref[0:32, 64:128])
    qb = dot(turn[:, 32:64], gt_ref[32:64, 64:128])
    slot_a = jnp.maximum(pair - 1, 0)
    slot_b = jnp.minimum(pair + 1, 31)
    zero = jnp.zeros((64, 64), F32)
    halves = []
    for n in range(2):
        slot = 2 * row + n
        halves.append(jnp.where(slot == slot_a, qa, jnp.where(slot == slot_b, qb, zero)))
    acc_ref[...] = jnp.concatenate(halves, axis=1)


def back(gt, yh, yl):
    vmem = pl.BlockSpec(memory_space=pltpu.VMEM)
    return pl.pallas_call(
        back_kernel,
        out_shape=(
            jax.ShapeDtypeStruct((64, 2048), F32),
            jax.ShapeDtypeStruct((64, 128), F32),
        ),
        in_specs=[vmem, vmem, vmem],
        out_specs=(vmem, vmem),
        compiler_params=pltpu.CompilerParams(vmem_limit_bytes=LIMIT),
    )(gt, yh, yl)


def local(matrix):
    gt, yh, yl = front(pltpu.with_memory_space_constraint(matrix, pltpu.HBM))
    return back(gt, yh, yl)


def solution(mesh):
    in_specs = (P("pair", "row"),)
    out_specs = (P("pair", "row"), P("pair", "row"))
    return jax.shard_map(local, mesh=mesh, in_specs=in_specs, out_specs=out_specs, check_vma=False)
```

```python
import jax
import jax.numpy as jnp
from jax import lax
from jax.experimental import pallas as pl
from jax.experimental.pallas import tpu as pltpu
from jax.sharding import PartitionSpec as P

F32 = jnp.float32
BF16 = jnp.bfloat16
HIGH = lax.Precision.HIGHEST
MESH = pl.DeviceIdType.MESH
DOUBLES = 31
CHUNKS = 4
CHUNK = 2048 // CHUNKS
EARLY = 1
BREAKS = (0, 0, 3, 11, 20)
BREAK_2 = 28
LIMIT = 16 * 1024 * 1024
FAR_FIRST = (4, 3, 5, 2, 6, 1, 7)


def iota(shape, d):
    return lax.broadcasted_iota(jnp.int32, shape, d)


def lane_gather(x, idx):
    dims = lax.GatherDimensionNumbers(
        offset_dims=(), collapsed_slice_dims=(1,), start_index_map=(1,),
        operand_batching_dims=(0,), start_indices_batching_dims=(0,))
    return lax.gather(x, idx[..., None], dims, (1, 1), mode=lax.GatherScatterMode.PROMISE_IN_BOUNDS)


def dot(a, b):
    return jnp.dot(a, b, precision=HIGH, preferred_element_type=F32)


def dot_tn(a, b):
    return lax.dot_general(a, b, (((0,), (0,)), ((), ())), precision=HIGH, preferred_element_type=F32)


def dot_nt(a, b):
    return lax.dot_general(a, b, (((1,), (1,)), ((), ())), precision=HIGH, preferred_element_type=F32)


def angle(gpp, gqq, gpq):
    d = gqq - gpp
    ad = jnp.abs(d)
    k = jnp.where(ad < 1e-9, F32(2.0 ** 50), jnp.where(ad > 1e9, F32(2.0 ** -80), F32(1.0)))
    k = jnp.where(ad < 1e-22, F32(2.0 ** 100), k)
    ad = ad * k
    square = ad * ad
    half = jnp.where(d >= 0, 0.5, -0.5).astype(F32)
    b = jnp.minimum(jnp.maximum(gpq * (k + k), -1e18), 1e18)
    h = square + b * b
    r = h * lax.rsqrt(h)
    hu = 0.5 * (ad + r)
    w = lax.rsqrt(r * hu)
    s = (b * half) * w
    return hu * w, s, s * (r * w) * gpq


def ssum(x):
    x = x + pltpu.roll(x, 4, 0)
    x = x + pltpu.roll(x, 2, 0)
    return x + pltpu.roll(x, 1, 0)


def shift(p, q, first, last):
    up = pltpu.roll(p[0], 7, 0)
    down = pltpu.roll(q[3], 1, 0)
    new_p = [jnp.where(first, p[0], p[1]), p[2], p[3], jnp.where(last, q[3], up)]
    new_q = [jnp.where(first, p[1], down), q[0], q[1], q[2]]
    return new_p, new_q


def step(_, carry):
    lane = iota((8, 128), 1)
    sub = iota((8, 128), 0)
    first, last = sub == 0, sub == 7
    wide = lane >= 64
    p, q, dp, dq, rq = [list(carry[4 * n:4 * n + 4]) for n in range(5)]
    pos, mate = carry[20], carry[21]
    near = jnp.where(wide, 127, jnp.minimum(pos, 63 - pos))
    sign = jnp.where(pos < 32, -1.0, 1.0).astype(F32)
    partner = jnp.where(mate == lane, 0, mate)
    partner = jnp.where(wide, lane, partner)
    c, s, cs, ss = [], [], [], []
    for v in range(4):
        cv, sv, fix = angle(dp[v], dq[v], lane_gather(p[v], rq[v]))
        dp[v] = dp[v] - fix
        dq[v] = dq[v] + fix
        hit = near == v + 4 * sub
        c.append(cv)
        s.append(sv)
        cs.append(jnp.where(hit, cv, 0.0))
        ss.append(jnp.where(hit, sv, 0.0))
    cc = ssum((cs[0] + cs[1]) + (cs[2] + cs[3])) + jnp.where(wide, 1.0, 0.0)
    sc = ssum((ss[0] + ss[1]) + (ss[2] + ss[3])) * sign
    for v in range(4):
        pm = lane_gather(p[v], partner)
        qm = lane_gather(q[v], partner)
        a, b = p[v], q[v]
        p[v] = (c[v] * a - s[v] * b) * cc + (c[v] * pm - s[v] * qm) * sc
        q[v] = (s[v] * a + c[v] * b) * cc + (s[v] * pm + c[v] * qm) * sc
    p, q = shift(p, q, first, last)
    dp, dq = shift(dp, dq, first, last)
    rq = [jnp.where(x == 63, 1, x + 1) for x in rq]
    pos = jnp.where(pos == 0, 0, jnp.where(pos == 1, 63, pos - 1))
    mate = mate + jnp.where(lane == 0, 1, 2)
    mate = jnp.where(mate > 63, mate - 63, mate)
    return tuple(p + q + dp + dq + rq + [pos, mate])


def row_order():
    r = iota((64, 64), 0)
    n = iota((64, 64), 1)
    k = r & 31
    i = (k >> 3) + 4 * (k & 7)
    return jnp.where(n == jnp.where(r >= 32, 63 - i, i), 1.0, 0.0).astype(F32)


def sweep_start(state):
    lane = iota((8, 128), 1)
    sub = iota((8, 128), 0)
    p = [state[8 * v:8 * v + 8] for v in range(4)]
    q = [state[32 + 8 * v:40 + 8 * v] for v in range(4)]
    rq = [63 - (v + 4 * sub) for v in range(4)]
    dp = [lane_gather(p[v], v + 4 * sub) for v in range(4)]
    dq = [lane_gather(q[v], rq[v]) for v in range(4)]
    mate = jnp.where(lane >= 63, 63, 63 - lane)
    carry = step(0, tuple(p + q + dp + dq + rq + [lane, mate]))
    return carry + (jnp.full((8, 128), 65, jnp.int32),)


def wrap(x):
    return jnp.where(x > 63, x - 63, x)


def spread(near, values, sub):
    hits = [jnp.where(near == v + 4 * sub, values[v], 0.0) for v in range(4)]
    return ssum((hits[0] + hits[1]) + (hits[2] + hits[3]))


def coefs(pos, c, s, sub, wide):
    near = jnp.where(wide, 127, jnp.minimum(pos, 63 - pos))
    sign = jnp.where(pos < 32, -1.0, 1.0).astype(F32)
    return spread(near, c, sub) + jnp.where(wide, 1.0, 0.0), spread(near, s, sub) * sign


def next_pos(pos):
    return jnp.where(pos == 0, 0, jnp.where(pos == 1, 63, pos - 1))


def partner_of(mate, lane, wide):
    return jnp.where(wide, lane, jnp.where(mate == lane, 0, mate))


def turn_rows(p, q, c, s):
    a = [c[v] * p[v] - s[v] * q[v] for v in range(4)]
    b = [s[v] * p[v] + c[v] * q[v] for v in range(4)]
    return a, b


def blend(rows, others, cc, sc):
    return [x * cc + y * sc for x, y in zip(rows, others)]


def double_step(_, carry):
    lane = iota((8, 128), 1)
    sub = iota((8, 128), 0)
    first, last = sub == 0, sub == 7
    wide = lane >= 64
    p, q, dp, dq, rq = [list(carry[4 * n:4 * n + 4]) for n in range(5)]
    pos, mate, twice = carry[20], carry[21], carry[22]
    pos2 = next_pos(pos)
    mate2 = wrap(mate + jnp.where(lane == 0, 1, 2))
    one = partner_of(mate, lane, wide)
    two = partner_of(mate2, lane, wide)
    both = lane_gather(one, two)

    g = [lane_gather(p[v], rq[v]) for v in range(4)]
    pz, qz = list(p), list(q)
    pz[1] = jnp.where(first, pltpu.roll(q[3], 1, 0), p[1])
    qz[1] = jnp.where(first, pltpu.roll(p[3], 1, 0), q[1])
    ra, rb = [], []
    for v in range(4):
        step_by = 2
        if v == 0:
            step_by = jnp.where(first, 1, 2)
        if v == 1:
            step_by = jnp.where(first, 34, 2)
        n = wrap(rq[v] + step_by)
        m = wrap(twice - n)
        m = jnp.where(m == n, 0, m)
        ra.append((lane_gather(pz[v], n), lane_gather(qz[v], n)))
        rb.append((lane_gather(pz[v], m), lane_gather(qz[v], m)))
    pa = [lane_gather(x, one) for x in p]
    qa = [lane_gather(x, one) for x in q]
    pb = [lane_gather(x, two) for x in p]
    qb = [lane_gather(x, two) for x in q]
    pc = [lane_gather(x, both) for x in p]
    qc = [lane_gather(x, both) for x in q]

    c, s = [], []
    for v in range(4):
        cv, sv, fix = angle(dp[v], dq[v], g[v])
        dp[v] = dp[v] - fix
        dq[v] = dq[v] + fix
        c.append(cv)
        s.append(sv)
    dp, dq = shift(dp, dq, first, last)

    c2r, c3r = pltpu.roll(c[2], 1, 0), pltpu.roll(c[3], 1, 0)
    s2r, s3r = pltpu.roll(s[2], 1, 0), pltpu.roll(s[3], 1, 0)
    cz = [c[0], jnp.where(first, c3r, c[1]), c[2], c[3]]
    sz = [s[0], jnp.where(first, -s3r, s[1]), s[2], s[3]]
    cn = [jnp.where(first, c[1], c2r), jnp.where(first, c2r, c3r), c[0], c[1]]
    sn = [jnp.where(first, -s[1], s2r), jnp.where(first, s2r, s3r), s[0], s[1]]
    gs = []
    for v in range(4):
        at_n = cz[v] * ra[v][0] - sz[v] * ra[v][1]
        at_m = cz[v] * rb[v][0] - sz[v] * rb[v][1]
        gs.append(at_n * cn[v] + at_m * sn[v])
    g2 = [jnp.where(first, gs[0], gs[1]), gs[2], gs[3],
          jnp.where(last, pltpu.roll(gs[1], 7, 0), pltpu.roll(gs[0], 7, 0))]
    c2, s2 = [], []
    for v in range(4):
        cv, sv, fix = angle(dp[v], dq[v], g2[v])
        dp[v] = dp[v] - fix
        dq[v] = dq[v] + fix
        c2.append(cv)
        s2.append(sv)
    dp, dq = shift(dp, dq, first, last)

    cc, sc = coefs(pos, c, s, sub, wide)
    far = 63 - pos2
    far = jnp.where(far == 0, 0, jnp.where(far == 63, 1, far + 1))
    ccp, scp = coefs(far, c, s, sub, wide)
    p1, q1 = turn_rows(p, q, c, s)
    p1a, q1a = turn_rows(pa, qa, c, s)
    p1b, q1b = turn_rows(pb, qb, c, s)
    p1c, q1c = turn_rows(pc, qc, c, s)
    p, q = shift(blend(p1, p1a, cc, sc), blend(q1, q1a, cc, sc), first, last)
    pm, qm = shift(blend(p1b, p1c, ccp, scp), blend(q1b, q1c, ccp, scp), first, last)
    cc2, sc2 = coefs(pos2, c2, s2, sub, wide)
    p2, q2 = turn_rows(p, q, c2, s2)
    p2m, q2m = turn_rows(pm, qm, c2, s2)
    p, q = shift(blend(p2, p2m, cc2, sc2), blend(q2, q2m, cc2, sc2), first, last)
    rq = [wrap(wrap(x + 1) + 1) for x in rq]
    mate = wrap(mate2 + jnp.where(lane == 0, 1, 2))
    twice = jnp.where(twice + 4 > 126, twice - 59, twice + 4)
    return tuple(p + q + dp + dq + rq + [next_pos(pos2), mate, twice])


def split(x):
    hi = x.astype(BF16)
    return hi, (x - hi.astype(F32)).astype(BF16)


def gram_of(ah, al, bh, bl):
    dims = (((1,), (1,)), ((), ()))
    rows = ah.shape[0]
    both = lax.dot_general(jnp.concatenate([ah, al], axis=0), bh, dims, preferred_element_type=F32)
    return (both[:rows] + both[rows:]) + lax.dot_general(ah, bl, dims, preferred_element_type=F32)


def product(ah, al, bh, bl):
    rows = ah.shape[0]
    both = jnp.dot(jnp.concatenate([ah, al], axis=0), bh, preferred_element_type=F32)
    return (both[:rows] + both[rows:]) + jnp.dot(ah, bl, preferred_element_type=F32)


def pack(g):
    return jnp.concatenate([g[:32], g[32:]], axis=1)


def unpack(p):
    return jnp.concatenate([p[:, :64], p[:, 64:]], axis=0)


def sum_chips(chips):
    return ((chips[0] + chips[1]) + (chips[2] + chips[3])) + ((chips[4] + chips[5]) + (chips[6] + chips[7]))


def front_kernel(x_in, gt_ref, yh_ref, yl_ref, x_ref, part, mate, chips, part2, mate2, chips2,
                 xs, hi, lo, pay, came, send_sem, recv_sem, local_sem, up_sem, down_sem):
    pair = lax.axis_index("pair")
    row = lax.axis_index("row")
    z = row // 2
    core = row % 2
    partner = (pair, 2 * z + (1 - core))
    others = [(pair, 2 * ((z + d) % 8) + core) for d in FAR_FIRST]
    ahead = ((pair + 1) % 32, row)
    behind = ((pair + 31) % 32, row)
    has_ahead = pair < 31
    has_behind = pair > 0

    def send(src, dst, slot, device):
        return pltpu.make_async_remote_copy(
            src_ref=src, dst_ref=dst, send_sem=send_sem.at[slot], recv_sem=recv_sem.at[slot],
            device_id=device, device_id_type=MESH)

    def start_both(forward, backward):
        pl.when(has_ahead)(forward.start)
        pl.when(has_behind)(backward.start)

    def wait_both(forward, backward):
        pl.when(has_behind)(forward.wait_recv)
        pl.when(has_ahead)(backward.wait_recv)
        pl.when(has_ahead)(forward.wait_send)
        pl.when(has_behind)(backward.wait_send)

    load = pltpu.make_async_copy(x_in, x_ref, local_sem)
    load.start()
    barrier = pltpu.get_barrier_semaphore()

    def greet(device):
        pl.semaphore_signal(barrier, inc=1, device_id=device, device_id_type=MESH)

    pl.when(has_ahead)(lambda: greet(ahead))
    pl.when(has_behind)(lambda: greet(behind))
    above = (pair, 2 * ((z + 1) % 8) + core)
    below = (pair, 2 * ((z + 7) % 8) + core)
    for device in (partner, above, below):
        greet(device)
    load.wait()
    xh, xl = split(x_ref[...])
    part[...] = pack(gram_of(xh, xl, xh, xl))
    pl.semaphore_wait(barrier, 3 + jnp.where(has_ahead, 1, 0) + jnp.where(has_behind, 1, 0))

    blocks = []
    for n in range(CHUNKS):
        lanes = pl.ds(n * CHUNK, CHUNK)
        forward = send(x_in.at[:, lanes], xs.at[0:64, lanes], 18 + 2 * n, ahead)
        backward = send(x_in.at[:, lanes], xs.at[64:128, lanes], 19 + 2 * n, behind)
        start_both(forward, backward)
        blocks.append((forward, backward))
    def tell(sem, n, device):
        pl.semaphore_signal(sem.at[n], inc=1, device_id=device, device_id_type=MESH)

    tell(up_sem, 0, above)
    tell(down_sem, 0, below)
    to_mate = send(part, mate, 0, partner)
    to_mate.start()
    to_mate.wait()
    pl.semaphore_wait(up_sem.at[0], 1)
    tell(up_sem, 1, above)
    pl.semaphore_wait(down_sem.at[0], 1)
    tell(down_sem, 1, below)
    pl.semaphore_wait(up_sem.at[1], 1)
    tell(up_sem, 2, above)
    pl.semaphore_wait(down_sem.at[1], 1)
    pl.semaphore_wait(up_sem.at[2], 1)
    chips[z] = part[...] + mate[...]
    copies = [send(chips.at[z], chips.at[z], 1 + n, device) for n, device in enumerate(others)]
    for copy in copies:
        copy.start()

    def take(n, cross):
        wait_both(*blocks[n])
        lanes = pl.ds(n * CHUNK, CHUNK)

        @pl.when(pair == 0)
        def _():
            xs[0:64, lanes] = x_ref[:, lanes]

        @pl.when(pair == 31)
        def _():
            xs[64:128, lanes] = x_ref[:, lanes]

        ah, al = split(xs[0:64, lanes])
        bh, bl = split(xs[64:128, lanes])
        hi[0:64, lanes] = ah
        hi[64:128, lanes] = bh
        lo[0:64, lanes] = al
        lo[64:128, lanes] = bl
        return cross + gram_of(ah, al, bh, bl)

    cross = jnp.zeros((64, 64), F32)
    for n in range(EARLY):
        cross = take(n, cross)
    for copy in copies:
        copy.wait()
    order = row_order()
    gram = unpack(sum_chips(chips))
    carry = sweep_start(jnp.concatenate([dot(order, gram), order], axis=1))
    for n in range(EARLY, CHUNKS):
        if BREAKS[n] < BREAKS[n + 1]:
            carry = lax.fori_loop(BREAKS[n], BREAKS[n + 1], double_step, carry)
        cross = take(n, cross)
    part2[...] = pack(cross)
    to_mate2 = send(part2, mate2, 8, partner)
    to_mate2.start()
    carry = lax.fori_loop(BREAKS[CHUNKS], BREAK_2, double_step, carry)
    to_mate2.wait()
    chips2[z] = part2[...] + mate2[...]
    copies2 = [send(chips2.at[z], chips2.at[z], 9 + n, device) for n, device in enumerate(others)]
    for copy in copies2:
        copy.start()
    carry = lax.fori_loop(BREAK_2, DOUBLES, double_step, carry)

    upper = jnp.concatenate(carry[0:4], axis=0)
    lower = jnp.concatenate(carry[4:8], axis=0)
    top_order = order[0:32, 0:32]
    bottom_order = order[32:64, 32:64]
    flip = dot_nt(top_order, bottom_order)
    pay[0] = upper
    pay[1] = lower

    @pl.when(pair == 0)
    def _():
        pay[0] = dot(flip, lower)

    t_forward = send(pay.at[0], came.at[0], 16, ahead)
    t_backward = send(pay.at[1], came.at[1], 17, behind)
    start_both(t_forward, t_backward)
    turned = dot(flip, upper)
    wait_both(t_forward, t_backward)
    a = jnp.where(pair == 0, upper, came[0])
    b = jnp.where(pair == 31, turned, came[1])
    ta = a[:, 64:128]
    tb = b[:, 64:128]
    ta_flat = dot_tn(top_order, ta)
    tb_flat = dot_tn(bottom_order, tb)
    da = jnp.where(pair == 1, a[:, 32:64], a[:, 0:32])
    db = jnp.where(pair == 31, b[:, 0:32], b[:, 32:64])
    tah, tal = split(ta_flat)
    tbh, tbl = split(tb_flat)
    for n in range(CHUNKS):
        lanes = pl.ds(n * CHUNK, CHUNK)
        yh_ref[0:32, lanes], yl_ref[0:32, lanes] = split(product(tah, tal, hi[0:64, lanes], lo[0:64, lanes]))
        yh_ref[32:64, lanes], yl_ref[32:64, lanes] = split(product(tbh, tbl, hi[64:128, lanes], lo[64:128, lanes]))
    for copy in copies2:
        copy.wait()
    cross = unpack(sum_chips(chips2))
    off = dot_nt(dot(ta, cross), tb_flat)
    off_t = dot_nt(dot_nt(tb, cross), ta_flat)
    gt_ref[0:32] = jnp.concatenate([da, off, ta_flat], axis=1)
    gt_ref[32:64] = jnp.concatenate([off_t, db, tb_flat], axis=1)


def front(matrix):
    vmem = pl.BlockSpec(memory_space=pltpu.VMEM)
    small = pltpu.VMEM((32, 128), F32)
    many = pltpu.VMEM((8, 32, 128), F32)
    return pl.pallas_call(
        front_kernel,
        out_shape=(
            jax.ShapeDtypeStruct((64, 128), F32),
            jax.ShapeDtypeStruct((64, 2048), BF16),
            jax.ShapeDtypeStruct((64, 2048), BF16),
        ),
        in_specs=[pl.BlockSpec(memory_space=pltpu.HBM)],
        out_specs=(vmem, vmem, vmem),
        scratch_shapes=[
            pltpu.VMEM((64, 2048), F32),
            small, small, many, small, small, many,
            pltpu.VMEM((128, 2048), F32),
            pltpu.VMEM((128, 2048), BF16),
            pltpu.VMEM((128, 2048), BF16),
            pltpu.VMEM((2, 32, 128), F32),
            pltpu.VMEM((2, 32, 128), F32),
            pltpu.SemaphoreType.DMA((18 + 2 * CHUNKS,)),
            pltpu.SemaphoreType.DMA((18 + 2 * CHUNKS,)),
            pltpu.SemaphoreType.DMA(()),
            pltpu.SemaphoreType.REGULAR((3,)),
            pltpu.SemaphoreType.REGULAR((2,)),
        ],
        compiler_params=pltpu.CompilerParams(
            collective_id=0, has_side_effects=True, vmem_limit_bytes=LIMIT),
    )(matrix)


def back_kernel(gt_ref, yh_ref, yl_ref, out_ref, acc_ref):
    pair = lax.axis_index("pair")
    row = lax.axis_index("row")
    order = row_order()
    carry = sweep_start(jnp.concatenate([gt_ref[:, 0:64], order], axis=1))
    carry = lax.fori_loop(0, DOUBLES, double_step, carry)
    vh, vl = split(jnp.concatenate(carry[0:8], axis=0)[:, 64:128])
    unorder = order.astype(BF16)
    dims = (((0,), (0,)), ((), ()))
    th = lax.dot_general(unorder, vh, dims, preferred_element_type=F32)
    tl = lax.dot_general(unorder, vl, dims, preferred_element_type=F32)
    out_ref[...] = product(th.astype(BF16), tl.astype(BF16), yh_ref[...], yl_ref[...])
    turn = th + tl
    qa = dot(turn[:, 0:32], gt_ref[0:32, 64:128])
    qb = dot(turn[:, 32:64], gt_ref[32:64, 64:128])
    slot_a = jnp.maximum(pair - 1, 0)
    slot_b = jnp.minimum(pair + 1, 31)
    zero = jnp.zeros((64, 64), F32)
    halves = []
    for n in range(2):
        slot = 2 * row + n
        halves.append(jnp.where(slot == slot_a, qa, jnp.where(slot == slot_b, qb, zero)))
    acc_ref[...] = jnp.concatenate(halves, axis=1)


def back(gt, yh, yl):
    vmem = pl.BlockSpec(memory_space=pltpu.VMEM)
    return pl.pallas_call(
        back_kernel,
        out_shape=(
            jax.ShapeDtypeStruct((64, 2048), F32),
            jax.ShapeDtypeStruct((64, 128), F32),
        ),
        in_specs=[vmem, vmem, vmem],
        out_specs=(vmem, vmem),
        compiler_params=pltpu.CompilerParams(vmem_limit_bytes=LIMIT),
    )(gt, yh, yl)


def local(matrix):
    gt, yh, yl = front(pltpu.with_memory_space_constraint(matrix, pltpu.HBM))
    return back(gt, yh, yl)


def solution(mesh):
    in_specs = (P("pair", "row"),)
    out_specs = (P("pair", "row"), P("pair", "row"))
    return jax.shard_map(local, mesh=mesh, in_specs=in_specs, out_specs=out_specs, check_vma=False)
```
